32 devices in a mesh: pipe: 4 (over y, core), expert: 4 (over z), dp: 2 (over x).
Axes of the slice: x: 2, y: 2, z: 4, core: 2. Of those that a mesh axis runs over, the one named last changes fastest.
Arguments:
- acts: bfloat16 [256, 3584], P(('pipe', 'expert', 'dp')), may hold values from -6 to 6
- cotangent: bfloat16 [256, 3584], P(('pipe', 'expert', 'dp')), may hold values from -6 to 6
- routes: int32 [256, 1], P(('pipe', 'expert', 'dp')), may hold values from 0 to 1; in each aligned block of 8 rows (0 to 7, 8 to 15, ...) at most 6 rows name the same one
- probs: bfloat16 [256, 1], P(('pipe', 'expert', 'dp')), may hold values from 0.19921875 to 1
- keep: int32 [4, 8], P('pipe', ('expert', 'dp')), may hold values 0 or 1
- w_gate: bfloat16 [4, 4, 3584, 512], P('pipe', 'expert', None, 'dp'), may hold values from -0.09375 to 0.09375
- w_up: bfloat16 [4, 4, 3584, 512], P('pipe', 'expert', None, 'dp'), may hold values from -0.09375 to 0.09375
- w_down: bfloat16 [4, 4, 512, 3584], P('pipe', 'expert', 'dp'), may hold values from -0.1875 to 0.1875
Outputs:
- layer_out: bfloat16 [256, 3584], P(('pipe', 'expert', 'dp'))
- grad_below: bfloat16 [256, 3584], P(('pipe', 'expert', 'dp'))
The draws below stay inside these ranges and needn't reach their ends.
Inputs may be any that keep to these rules, and one draw needn't show every extreme that they name: `routes`: the 1 expert of a token differ. Among the rows of one device no expert is named more than 6 times, and in every draw some device names some expert exactly 6 times.
All inputs are finite; a program needn't handle non-finite values. No bound on the sum of `keep` on one device may be relied on, other than what follows from the above.
Results may differ from the reference program's by a relative error of at most 0.0075.
Values may be sent and summed in bfloat16 or wider, within the bound.
No kernel may reach another device: no remote copies, remote signals or barrier semaphores. Data moves between devices by JAX's collectives and lax.ppermute only.
A program may use at most 64 MiB of HBM per device.

```python
import math
import jax
import jax.numpy as jnp
import numpy as np
from jax import lax

D = 3584
FF = 1024
TOK_DEV = 8
TOPK = 1
EXPERTS = 2
CAP = 6
ROWS = 256
N_PIPE = 4
N_EXPERT = 4
N_DP = 2


def place_ends(values, key, smallest, top_value):
    shape = values.shape
    spot = [jax.random.randint(jax.random.fold_in(key, axis), (), 0, shape[axis]) for axis in range(len(shape))]
    values = values.at[tuple(spot)].set(smallest)
    longest = shape.index(max(shape))
    spot[longest] = (spot[longest] + 1) % shape[longest]
    return values.at[tuple(spot)].set(top_value)


def block_scale(key, dims, cuts, smallest, top_value):
    def one(dim, parts):
        steps = jax.random.uniform(jax.random.fold_in(jax.random.fold_in(key, 6), dim), (parts,), jnp.float32, smallest / len(cuts), top_value / len(cuts))
        return jnp.repeat(jnp.exp(steps), dims[dim] // parts).reshape((-1,) + (1,) * (len(dims) - dim - 1))

    gain = one(*cuts[0])
    for cut in cuts[1:]:
        gain = gain * one(*cut)
    return gain


def deal_out(stream_key, own, number, rows, amount, top, bound, lean):
    ranking = jax.random.permutation(stream_key, amount)
    crowded, ordinary = shares(amount, rows * top, bound, lean, True), shares(amount, rows * top, bound, lean, False)
    places = jnp.arange(amount)

    def named(lengths, offset_by):
        used = int((lengths > 0).sum())
        fixed = max(1, used // 4)
        passed = fixed + (places - fixed + offset_by * (used - fixed)) % max(1, amount - fixed)
        return jnp.zeros((amount,), jnp.int32).at[ranking[jnp.where(places < fixed, places, passed)]].set(jnp.asarray(lengths, jnp.int32))

    lengths = jnp.where(number % 4 == 0, named(crowded, number // 4), named(ordinary, number - number // 4 - 1))
    mixed = jax.random.permutation(jax.random.fold_in(own, 3), amount)
    source_of, taker = mixed[0:amount // 2 * 2:2], mixed[1:amount // 2 * 2:2]
    margin = jnp.minimum(lengths[source_of] - 1, bound - lengths[taker]) // 2
    margin = jnp.where((source_of == ranking[0]) | (taker == ranking[0]) | (lengths[taker] == 0), 0, jnp.maximum(margin, 0))
    passed = jax.random.randint(jax.random.fold_in(own, 4), (amount // 2,), 0, 1 << 20) % (margin + 1)
    lengths = lengths.at[source_of].add(-passed).at[taker].add(passed)
    items = jnp.searchsorted(jnp.cumsum(lengths), jnp.arange(rows * top), side="right").astype(jnp.int32)
    listing = items.reshape(top, rows).T
    listing = listing[jax.random.permutation(jax.random.fold_in(own, 1), rows)]
    offset_by = jax.random.randint(jax.random.fold_in(own, 2), (rows, 1), 0, top)
    return jnp.take_along_axis(listing, (jnp.arange(top)[None, :] + offset_by) % top, axis=1)


def shares(number_of, total, bound, skew, full):
    portions = [(1 << 20) // math.isqrt(standing ** skew) + 1 for standing in range(1, number_of + 1)]
    largest = bound if full else min(bound, max(-(-total // number_of), total * portions[0] // sum(portions)))
    least = 1 if total - largest >= number_of - 1 else 0
    holding, spare = [largest] + [least] * (number_of - 1), total - largest - least * (number_of - 1)
    while spare > 0:
        free = [i for i in range(1, number_of) if holding[i] < largest] or [i for i in range(1, number_of) if holding[i] < bound]
        pool, left = sum([portions[i] for i in free]), spare
        for i in free:
            extra = min(bound - holding[i], max(1, left * portions[i] // pool), spare)
            holding[i] = holding[i] + extra
            spare = spare - extra
    return np.array(holding)


def bell_draw(rng, shape, spread, limit, shards=(), held_as=jnp.bfloat16):
    factor_of = block_scale(rng, shape, shards, -0.22, 0.18) if shards else 1.0
    entries = jax.random.normal(rng, shape, jnp.float32) * spread * factor_of
    return jnp.minimum(jnp.maximum(entries, -limit), limit).astype(held_as)


def setup_inputs(seed: int = 0) -> dict:
    keys = jax.random.split(jax.random.key(seed), 9)
    acts = bell_draw(keys[0], (ROWS, D), 1.0, 6.0, ((0, 32),))
    cotangent = bell_draw(keys[1], (ROWS, D), 1.0, 6.0, ((0, 32),))
    routes_keys = jax.random.split(jax.random.fold_in(keys[2], 1), ROWS // TOK_DEV)
    routes_turns = jax.random.permutation(jax.random.fold_in(keys[2], 3), ROWS // TOK_DEV)
    routes = jax.vmap(lambda own, number: deal_out(jax.random.fold_in(keys[2], 2), own, number, TOK_DEV, EXPERTS, TOPK, CAP, 2))(routes_keys, routes_turns).reshape((ROWS, TOPK))
    probs = jnp.clip(0.19921875 + 0.80078125 * jax.random.uniform(keys[3], (ROWS, TOPK), jnp.float32) ** block_scale(keys[3], (ROWS, TOPK), ((0, 32),), -0.2, 0.2), 0.19921875, 1.0).astype(jnp.bfloat16)
    keep = place_ends((jax.random.randint(keys[4], (N_PIPE, N_EXPERT * N_DP), 0, 4) < 3).astype(jnp.int32), jax.random.fold_in(keys[4], 1), 0, 1)
    w_gate = bell_draw(keys[5], (N_PIPE, N_EXPERT, D, FF // 2), D ** -0.5, 0.09375, ((0, 4), (1, 4), (3, 2)))
    w_up = bell_draw(keys[6], (N_PIPE, N_EXPERT, D, FF // 2), D ** -0.5, 0.09375, ((0, 4), (1, 4), (3, 2)))
    w_down = bell_draw(keys[7], (N_PIPE, N_EXPERT, FF // 2, D), FF ** -0.5, 0.1875, ((0, 4), (1, 4), (2, 2)))
    return {"acts": acts, "cotangent": cotangent, "routes": routes, "probs": probs, "keep": keep, "w_gate": w_gate, "w_up": w_up, "w_down": w_down}


def expert_half(section_acts, section_cot, gate_half, up_half, down_half):
    gate_pre = jnp.dot(section_acts, gate_half, preferred_element_type=jnp.float32)
    up_pre = jnp.dot(section_acts, up_half, preferred_element_type=jnp.float32)
    squash = jax.nn.sigmoid(gate_pre)
    hidden = (gate_pre * squash * up_pre).astype(jnp.bfloat16)
    grad_hidden = jnp.dot(section_cot, down_half.T, preferred_element_type=jnp.float32)
    grad_gate = (grad_hidden * up_pre * squash * (1.0 + gate_pre * (1.0 - squash))).astype(jnp.bfloat16)
    grad_up = (grad_hidden * gate_pre * squash).astype(jnp.bfloat16)
    row_count = section_acts.shape[0]
    hidden_groups = hidden.reshape(row_count, N_DP, -1).astype(jnp.float32)
    down_groups = down_half.reshape(N_DP, -1, D).astype(jnp.float32)
    part_out = jnp.einsum("nrf,rfd->rnd", hidden_groups, down_groups).astype(jnp.bfloat16)
    gate_weight_groups = gate_half.reshape(D, N_DP, -1).astype(jnp.float32)
    up_weight_groups = up_half.reshape(D, N_DP, -1).astype(jnp.float32)
    gate_gradient_parts = grad_gate.reshape(row_count, N_DP, -1).astype(jnp.float32)
    up_gradient_parts = grad_up.reshape(row_count, N_DP, -1).astype(jnp.float32)
    partial_gradient = (jnp.einsum("ame,ome->mao", gate_gradient_parts, gate_weight_groups)
                 + jnp.einsum("ame,ome->mao", up_gradient_parts, up_weight_groups)).astype(jnp.bfloat16)
    half_out = jnp.sum(part_out.astype(jnp.float32), axis=0).astype(jnp.bfloat16)
    half_grad = jnp.sum(partial_gradient.astype(jnp.float32), axis=0).astype(jnp.bfloat16)
    return half_out, half_grad


def reference(acts, cotangent, routes, probs, keep, w_gate, w_up, w_down):
    section_rows = ROWS // N_PIPE
    all_acts = acts.reshape(N_PIPE, section_rows, D)
    all_cot = cotangent.reshape(N_PIPE, section_rows, D)
    all_routes = routes.reshape(N_PIPE, section_rows, TOPK)
    all_probs = probs.reshape(N_PIPE, section_rows, TOPK)

    def per_section(packed):
        section_acts, section_cot, section_routes, section_probs, section_keep, gate_w, up_w, down_w = packed
        gate_four = gate_w.reshape(EXPERTS, 2, D, -1)
        up_four = up_w.reshape(EXPERTS, 2, D, -1)
        down_four = down_w.reshape(EXPERTS, 2, -1, D)

        def per_expert(carry, item):
            mixed_out, mixed_grad = carry
            gate_pair, up_weight_pair, down_pair, expert_id = item
            out_low, grad_low = expert_half(section_acts, section_cot, gate_pair[0], up_weight_pair[0], down_pair[0])
            out_high, grad_high = expert_half(section_acts, section_cot, gate_pair[1], up_weight_pair[1], down_pair[1])
            expert_out = (out_low.astype(jnp.float32) + out_high.astype(jnp.float32)).astype(jnp.bfloat16)
            expert_grad = (grad_low.astype(jnp.float32) + grad_high.astype(jnp.float32)).astype(jnp.bfloat16)
            weight_col = jnp.sum(jnp.where(section_routes == expert_id, section_probs.astype(jnp.float32), jnp.float32(0.0)), axis=1)
            mixed_out = mixed_out + weight_col[:, None] * expert_out.astype(jnp.float32)
            mixed_grad = mixed_grad + weight_col[:, None] * expert_grad.astype(jnp.float32)
            return (mixed_out, mixed_grad), None

        start = (jnp.zeros((section_rows, D), jnp.float32), jnp.zeros((section_rows, D), jnp.float32))
        ids = jnp.arange(EXPERTS, dtype=jnp.int32)
        (mixed_out, mixed_grad), unused = lax.scan(per_expert, start, (gate_four, up_four, down_four, ids))
        keep_scale = jnp.repeat(section_keep.astype(jnp.float32), TOK_DEV)[:, None]
        layer_out = (section_acts.astype(jnp.float32) + keep_scale * mixed_out).astype(jnp.bfloat16)
        section_grad = (section_cot.astype(jnp.float32) + keep_scale * mixed_grad).astype(jnp.bfloat16)
        return layer_out, section_grad

    outs, grads = lax.map(per_section, (all_acts, all_cot, all_routes, all_probs, keep, w_gate, w_up, w_down))
    below = jnp.concatenate([grads[1:], jnp.zeros_like(grads[:1])], axis=0)
    return outs.reshape(ROWS, D), below.reshape(ROWS, D)
```

```python
import jax
import jax.numpy as jnp
from jax import lax
from jax.sharding import PartitionSpec as P


def rotate(shard, axis, by):
    count = lax.axis_size(axis)
    return lax.ppermute(shard, axis, [(i, (i + by) % count) for i in range(count)])


def flip(shard, axis):
    count = lax.axis_size(axis)
    return lax.ppermute(shard, axis, [(i, i ^ 1) for i in range(count)])


def from_behind(shard, axis, by):
    count = lax.axis_size(axis)
    pairs = [(i, i + by) for i in range(count) if 0 <= i + by < count]
    return lax.ppermute(shard, axis, pairs)


def rounded(x):
    return x.astype(jnp.bfloat16)


def dot(a, b, dims=(((1,), (0,)), ((), ()))):
    return lax.dot_general(a, b, dims, preferred_element_type=jnp.float32)


CROSS = (((1,), (1,)), ((), ()))


def gather_rows(hots, rows):
    cap = hots.shape[1]
    packed = [rounded(dot(hot, rows)) for hot in hots]
    parts = [packed[0]] + [rotate(packed[k], "expert", 2 * k) for k in range(1, len(packed))]
    own = jnp.concatenate(parts, axis=0)
    both = jnp.concatenate([own, flip(own, "expert")], axis=0)
    r = lax.axis_size("dp")
    return jnp.concatenate([both] + [rotate(both, "dp", k) for k in range(1, r)], axis=0)


def return_rows(partial, cap):
    r = lax.axis_size("dp")
    experts = lax.axis_size("expert") // 2
    blocks = partial.reshape(r, 2 * experts * cap, partial.shape[1])
    total = blocks[0].astype(jnp.float32)
    for k in range(1, r):
        total = total + rotate(blocks[k], "dp", -k).astype(jnp.float32)
    half = rounded(total).reshape(2, experts * cap, partial.shape[1])
    whole = rounded(half[0].astype(jnp.float32) + flip(half[1], "expert").astype(jnp.float32))
    whole = whole.reshape(experts, cap, partial.shape[1])
    back = [whole[0]] + [rotate(whole[k], "expert", -2 * k) for k in range(1, experts)]
    return jnp.concatenate(back, axis=0)


def shards(acts, cotangent, routes, probs, keep, w_gate, w_up, w_down):
    n_expert = lax.axis_size("expert")
    experts = n_expert // 2
    token_count, width = acts.shape
    top_count = routes.shape[1]
    capacity = 2 * ((token_count * top_count * 5 + 8 * experts - 1) // (8 * experts))
    pair_count = token_count * top_count
    chosen = routes.reshape(pair_count)
    weights = probs.reshape(pair_count)
    expert_hot = (chosen[:, None] == jnp.arange(experts, dtype=jnp.int32)[None, :]).astype(jnp.int32)
    ranks = jnp.cumsum(expert_hot, axis=0) - 1
    placed = jnp.sum(expert_hot * ranks, axis=1)
    mine = lax.axis_index("expert") // 2
    distance = (chosen - mine + experts) % experts
    slot = distance * capacity + placed
    slot_hot = slot[:, None] == jnp.arange(experts * capacity, dtype=jnp.int32)[None, :]
    owner = jnp.arange(pair_count, dtype=jnp.int32) // top_count
    token_hot = rounded(owner[:, None] == jnp.arange(token_count, dtype=jnp.int32)[None, :])
    hots = rounded(dot(rounded(slot_hot).T, token_hot)).reshape(experts, capacity, token_count)
    weighted_hot = jnp.where(slot_hot, weights[:, None], jnp.zeros((), jnp.bfloat16))
    spread = rounded(dot(token_hot.T, weighted_hot))

    gate_cols, up_cols, down_rows = w_gate[0, 0], w_up[0, 0], w_down[0, 0]
    rows_in = gather_rows(hots, acts)
    rows_cot = gather_rows(hots, cotangent)
    gate_pre = dot(rows_in, gate_cols)
    up_pre = dot(rows_in, up_cols)
    squash = jax.nn.sigmoid(gate_pre)
    hidden = rounded(gate_pre * squash * up_pre)
    part_out = rounded(dot(hidden, down_rows))
    grad_hidden = dot(rows_cot, down_rows, CROSS)
    grad_gate = rounded(grad_hidden * up_pre * squash * (1.0 + gate_pre * (1.0 - squash)))
    grad_up = rounded(grad_hidden * gate_pre * squash)
    part_grad = rounded(dot(grad_gate, gate_cols, CROSS) + dot(grad_up, up_cols, CROSS))
    expert_out = return_rows(part_out, capacity)
    expert_grad = return_rows(part_grad, capacity)
    keep_scale = keep[0, 0].astype(jnp.float32)
    layer_out = rounded(acts.astype(jnp.float32) + keep_scale * dot(spread, expert_out))
    section_grad = rounded(cotangent.astype(jnp.float32) + keep_scale * dot(spread, expert_grad))
    return layer_out, from_behind(section_grad, "pipe", -1)


def solution(mesh):
    rows = P(("pipe", "expert", "dp"), None)
    return jax.shard_map(
        shards,
        mesh=mesh,
        in_specs=(
            rows,
            rows,
            rows,
            rows,
            P("pipe", ("expert", "dp")),
            P("pipe", "expert", None, "dp"),
            P("pipe", "expert", None, "dp"),
            P("pipe", "expert", "dp", None),
        ),
        out_specs=(rows, rows),
        check_vma=False,
    )
```

```python
import functools

import jax
import jax.numpy as jnp
from jax import lax
from jax.experimental import pallas as pl
from jax.experimental.pallas import tpu as pltpu
from jax.sharding import PartitionSpec as P

CROSS = (((1,), (1,)), ((), ()))
LANES = 128
TILE = 4
MIB = 1024 * 1024


def room(mib):
    return pltpu.CompilerParams(vmem_limit_bytes=mib * MIB)


def rounded(x):
    return x.astype(jnp.bfloat16)


def in_hbm(x):
    return pltpu.with_memory_space_constraint(x, pltpu.HBM)


def near_core(x):
    return pltpu.with_memory_space_constraint(x, pltpu.VMEM)


def dot(a, b, dims=(((1,), (0,)), ((), ()))):
    return lax.dot_general(a, b, dims, preferred_element_type=jnp.float32)


def to_member(shard, half, by):
    n, r = lax.axis_size("expert"), lax.axis_size("dp")
    pairs = [(e * r + d, (e ^ half) * r + (d + by) % r) for e in range(n) for d in range(r)]
    return lax.ppermute(shard, ("expert", "dp"), pairs)


def to_expert(shard, by):
    n = lax.axis_size("expert")
    return lax.ppermute(shard, "expert", [(e, (e + 2 * by) % n) for e in range(n)])


def to_below(shard):
    return lax.ppermute(shard, "pipe", [(p, p - 1) for p in range(1, lax.axis_size("pipe"))])


def pack_kernel(experts, cap, top, *refs):
    keep, stored, mix_out, blocks = refs[0], refs[1:5], refs[5], refs[6 : 6 + experts]
    held, sems = refs[6 + experts : -1], refs[-1]
    copies = [pltpu.make_async_copy(s, h, sems.at[i]) for i, (s, h) in enumerate(zip(stored, held))]
    for copy in copies:
        copy.start()
    routes, probs, acts, cot = held
    pairs = routes.shape[1]
    tokens = pairs // top
    copies[0].wait()
    chosen = jnp.broadcast_to(routes[...], (pairs, pairs))
    p = lax.broadcasted_iota(jnp.int32, (pairs, pairs), 0)
    q = lax.broadcasted_iota(jnp.int32, (pairs, pairs), 1)
    column = jnp.sum(jnp.where(p == q, chosen, 0), axis=1, keepdims=True)
    alike = column == chosen
    mine = lax.axis_index("expert") // 2

    def slot_of(expert, rank):
        far = expert - mine
        return jnp.where(far < 0, far + experts, far) * (2 * cap) + rank

    row_slot = slot_of(routes[...], jnp.sum(jnp.where(alike & (p < q), 1, 0), axis=0, keepdims=True))
    col_slot = slot_of(column, jnp.sum(jnp.where(alike & (q < p), 1, 0), axis=1, keepdims=True))
    slot = lax.broadcasted_iota(jnp.int32, (2 * experts * cap, pairs), 0)
    scatter = [jnp.where(slot == row_slot + t * cap, 1.0, 0.0) for t in range(2)]
    owner = None
    if top > 1:
        owner = lax.broadcasted_iota(jnp.int32, (tokens, pairs), 1) // top
        owner = rounded(jnp.where(owner == lax.broadcasted_iota(jnp.int32, (tokens, pairs), 0), 1.0, 0.0))
        scatter = [dot(rounded(s), owner, CROSS) for s in scatter]
    copies[2].wait()
    packed = dot(rounded(scatter[0]), acts[...])
    copies[3].wait()
    packed = rounded(packed + dot(rounded(scatter[1]), cot[...]))
    tiles = blocks[0].shape[0]
    for k, block in enumerate(blocks):
        for i in range(tiles):
            at = (k * tiles + i) * TILE
            block[i] = packed[at : at + TILE]
    copies[1].wait()
    weight = jnp.broadcast_to(probs[...].astype(jnp.float32) * keep[...].astype(jnp.float32), (pairs, pairs))
    weight = jnp.sum(jnp.where(p == q, weight, 0.0), axis=1, keepdims=True)
    slot = lax.broadcasted_iota(jnp.int32, (pairs, LANES), 1)
    for t in range(2):
        mix = jnp.where(slot == col_slot + t * cap, weight, 0.0)
        mix_out[t] = mix if owner is None else dot(owner, rounded(mix))


def fill(rows, at, ins, first, deep, tiles):
    spots = [(ref, b + first + i) for ref in ins for b in range(0, ref.shape[0], tiles) for i in range(deep)]
    for i in range(0, len(spots), 2):
        pair = [ref[b] for ref, b in spots[i : i + 2]]
        rows[at + i * TILE : at + (i + 2) * TILE] = jnp.concatenate(pair, axis=0)


def near_kernel(cap, count, *refs):
    stored, ins, (acts, cot), held, sems = refs[:3], refs[3 : 3 + count], refs[3 + count : 5 + count], refs[5 + count : -1], refs[-1]
    copies = [pltpu.make_async_copy(s, h, sems.at[i]) for i, (s, h) in enumerate(zip(stored, held))]
    for copy in copies:
        copy.start()
    deep, tiles = -(-cap // TILE), 2 * cap // TILE
    fill(acts, 0, ins, 0, deep, tiles)
    fill(cot, 0, ins, tiles - deep, deep, tiles)
    for copy in copies:
        copy.wait()


def expert_kernel(cap, count, w_gate, w_up, w_down, acts_in, cot_in, *refs):
    ins, outs, (acts, cot) = refs[:count], refs[count : 3 * count], refs[3 * count :]
    width = acts.shape[1]
    tiles = 2 * cap // TILE
    deep = -(-cap // TILE)
    lead = deep * TILE - cap
    places = [(out, b) for out in outs for b in range(0, out.shape[0], tiles)]
    tall = len(places) * deep * TILE
    near = count * deep * TILE
    fill(acts, near, ins, 0, deep, tiles)
    fill(cot, near, ins, tiles - deep, deep, tiles)
    gate_pre = dot(acts[...], w_gate[...])
    up_pre = dot(acts[...], w_up[...])
    grad_hidden = dot(cot[...], w_down[...], CROSS)
    if lead:
        grad_hidden = pltpu.roll(grad_hidden, tall - lead, 0)
    live = lax.broadcasted_iota(jnp.int32, gate_pre.shape, 0) % (deep * TILE) < cap
    squash = jax.nn.sigmoid(gate_pre)
    silu = gate_pre * squash
    hidden = rounded(jnp.where(live, silu * up_pre, 0.0))
    grad_gate = jnp.where(live, grad_hidden * up_pre * squash * (1.0 + gate_pre * (1.0 - squash)), 0.0)
    grad_up = jnp.where(live, grad_hidden * silu, 0.0)
    if lead:
        grad_gate, grad_up = pltpu.roll(grad_gate, lead, 0), pltpu.roll(grad_up, lead, 0)
    grad_gate, grad_up = rounded(grad_gate), rounded(grad_up)
    step = 512
    for at in range(0, width, step):
        cols = slice(at, at + step)
        out = dot(hidden, w_down[:, cols])
        grad = dot(grad_gate, w_gate[cols, :], CROSS) + dot(grad_up, w_up[cols, :], CROSS)
        for n, (ref, b) in enumerate(places):
            base = n * deep * TILE
            for i in range(tiles):
                parts = []
                if i < deep:
                    parts.append(out[base + i * TILE : base + (i + 1) * TILE])
                if i >= tiles - deep:
                    j = i - (tiles - deep)
                    parts.append(grad[base + j * TILE : base + (j + 1) * TILE])
                ref[b + i, :, cols] = rounded(sum(parts))


def sum_kernel(*refs):
    total = refs[0][...].astype(jnp.float32)
    for ref in refs[1:-1]:
        total = total + ref[...].astype(jnp.float32)
    refs[-1][...] = rounded(total)


def finish_kernel(which, cap, count, mix, base, *refs):
    own, back, result = refs[:count], refs[count:-1], refs[-1]
    tiles, deep = 2 * cap // TILE, -(-cap // TILE)
    total = base[...].astype(jnp.float32)
    weights = rounded(mix[which])
    for i in range(deep) if which == 0 else range(tiles - deep, tiles):
        rows = own[0][i].astype(jnp.float32)
        for ref in own[1:]:
            rows = rows + ref[i].astype(jnp.float32)
        for k, rows in enumerate([rounded(rows)] + [ref[i] for ref in back]):
            at = (k * tiles + i) * TILE
            total = total + dot(weights[:, at : at + TILE], rows)
    result[...] = rounded(total)


def shards(acts, cotangent, routes, probs, keep, w_gate, w_up, w_down):
    experts = lax.axis_size("expert") // 2
    r = lax.axis_size("dp")
    token_count, width = acts.shape
    top = routes.shape[1]
    capacity = 2 * ((token_count * top * 5 + 8 * experts - 1) // (8 * experts))
    pairs = token_count * top
    tiles = 2 * capacity // TILE
    hidden = w_gate.shape[-1]
    shape = jax.ShapeDtypeStruct
    block = pltpu.VMEM((tiles, TILE, width), jnp.bfloat16)
    rest = pltpu.VMEM(((experts - 1) * tiles, TILE, width), jnp.bfloat16)
    far_off, vmem = pl.BlockSpec(memory_space=pltpu.HBM), pl.BlockSpec(memory_space=pltpu.VMEM)
    inputs = (routes.reshape(1, pairs), probs.reshape(1, pairs), acts, cotangent)
    mix, *sent = pl.pallas_call(
        functools.partial(pack_kernel, experts, capacity, top),
        in_specs=[vmem] + [far_off] * 4,
        out_specs=[vmem] * (1 + experts),
        out_shape=[pltpu.VMEM((2, token_count, LANES), jnp.float32)] + [block] * experts,
        scratch_shapes=[pltpu.VMEM(x.shape, x.dtype) for x in inputs] + [pltpu.SemaphoreType.DMA((4,))],
        compiler_params=room(4),
        name="pack",
    )(keep, *map(in_hbm, inputs))

    members = [(half, by) for half in range(2) for by in range(r)]
    near = [sent[0]]
    got = [to_expert(sent[k], k) for k in range(1, experts)]
    near += [to_member(sent[0], half, by) for half, by in members[1:]]
    got = got[0] if experts == 2 else jnp.concatenate(got, axis=0)
    far = [got] + [to_member(got, half, by) for half, by in members[1:]]
    weights = (w_gate.reshape(width, hidden), w_up.reshape(width, hidden), w_down.reshape(hidden, width))
    tall = experts * 2 * r * (-(-capacity // TILE)) * TILE
    count = len(members)
    laid = pltpu.VMEM((tall, width), jnp.bfloat16)
    acts_rows, cot_rows, *held = pl.pallas_call(
        functools.partial(near_kernel, capacity, count),
        in_specs=[far_off] * 3 + [vmem] * count,
        out_specs=[vmem] * 5,
        out_shape=[laid] * 2 + [pltpu.VMEM(w.shape, w.dtype) for w in weights],
        scratch_shapes=[pltpu.SemaphoreType.DMA((3,))],
        compiler_params=room(4),
        name="near",
    )(*map(in_hbm, weights), *map(near_core, near))
    *parts, _, _ = pl.pallas_call(
        functools.partial(expert_kernel, capacity, count),
        in_specs=[vmem] * (5 + count),
        out_specs=[vmem] * (2 * count + 2),
        out_shape=[block] * count + [rest] * count + [laid] * 2,
        input_output_aliases={3: 2 * count, 4: 2 * count + 1},
        compiler_params=room(8),
        name="expert",
    )(*map(near_core, (*held, acts_rows, cot_rows, *far)))
    near, far = parts[:count], parts[count:]
    far = [far[0]] + [to_member(x, half, -by) for x, (half, by) in zip(far[1:], members[1:])]
    near = [near[0]] + [to_member(x, half, -by) for x, (half, by) in zip(near[1:], members[1:])]
    total = pl.pallas_call(sum_kernel, out_shape=rest, compiler_params=room(4), name="total")(*map(near_core, far))
    back = [to_expert(total[(k - 1) * tiles : k * tiles], -k) for k in range(1, experts)]
    layer_out, section_grad = [
        pl.pallas_call(
            functools.partial(finish_kernel, which, capacity, count),
            out_shape=shape(acts.shape, jnp.bfloat16) if which == 0 else pltpu.VMEM(acts.shape, jnp.bfloat16),
            compiler_params=room(4),
            name=name,
        )(*map(near_core, (mix, base, *near, *back)))
        for which, name, base in ((0, "out", acts), (1, "grad", cotangent))
    ]
    return layer_out, to_below(section_grad)


def solution(mesh):
    rows = P(("pipe", "expert", "dp"), None)
    return jax.shard_map(
        shards,
        mesh=mesh,
        in_specs=(
            rows,
            rows,
            rows,
            rows,
            P("pipe", ("expert", "dp")),
            P("pipe", "expert", None, "dp"),
            P("pipe", "expert", None, "dp"),
            P("pipe", "expert", "dp", None),
        ),
        out_specs=(rows, rows),
        check_vma=False,
    )
```

```python
import functools

import jax
import jax.numpy as jnp
from jax import lax
from jax.experimental import pallas as pl
from jax.experimental.pallas import tpu as pltpu
from jax.sharding import PartitionSpec as P

CROSS = (((1,), (1,)), ((), ()))
LANES = 128
TILE = 4
MIB = 1024 * 1024


def room(mib):
    return pltpu.CompilerParams(vmem_limit_bytes=mib * MIB)


def rounded(x):
    return x.astype(jnp.bfloat16)


def in_hbm(x):
    return pltpu.with_memory_space_constraint(x, pltpu.HBM)


def near_core(x):
    return pltpu.with_memory_space_constraint(x, pltpu.VMEM)


def dot(a, b, dims=(((1,), (0,)), ((), ()))):
    return lax.dot_general(a, b, dims, preferred_element_type=jnp.float32)


def to_member(shard, half, by):
    n, r = lax.axis_size("expert"), lax.axis_size("dp")
    pairs = [(e * r + d, (e ^ half) * r + (d + by) % r) for e in range(n) for d in range(r)]
    return lax.ppermute(shard, ("expert", "dp"), pairs)


def to_expert(shard, by):
    n = lax.axis_size("expert")
    return lax.ppermute(shard, "expert", [(e, (e + 2 * by) % n) for e in range(n)])


def to_below(shard):
    return lax.ppermute(shard, "pipe", [(p, p - 1) for p in range(1, lax.axis_size("pipe"))])


def pack_kernel(experts, cap, top, *refs):
    stored, mix_out, blocks = refs[:4], refs[4], refs[5 : 5 + experts]
    held, sems = refs[5 + experts : -1], refs[-1]
    copies = [pltpu.make_async_copy(s, h, sems.at[i]) for i, (s, h) in enumerate(zip(stored, held))]
    for copy in copies:
        copy.start()
    routes, probs, acts, cot = held
    pairs = routes.shape[1]
    tokens = pairs // top
    copies[0].wait()
    chosen = jnp.broadcast_to(routes[...], (pairs, pairs))
    p = lax.broadcasted_iota(jnp.int32, (pairs, pairs), 0)
    q = lax.broadcasted_iota(jnp.int32, (pairs, pairs), 1)
    column = jnp.sum(jnp.where(p == q, chosen, 0), axis=1, keepdims=True)
    alike = column == chosen
    mine = lax.axis_index("expert") // 2

    def slot_of(expert, rank):
        far = expert - mine
        return jnp.where(far < 0, far + experts, far) * (2 * cap) + rank

    row_slot = slot_of(routes[...], jnp.sum(jnp.where(alike & (p < q), 1, 0), axis=0, keepdims=True))
    col_slot = slot_of(column, jnp.sum(jnp.where(alike & (q < p), 1, 0), axis=1, keepdims=True))
    slot = lax.broadcasted_iota(jnp.int32, (2 * experts * cap, pairs), 0)
    scatter = [jnp.where(slot == row_slot + t * cap, 1.0, 0.0) for t in range(2)]
    owner = None
    if top > 1:
        owner = lax.broadcasted_iota(jnp.int32, (tokens, pairs), 1) // top
        owner = rounded(jnp.where(owner == lax.broadcasted_iota(jnp.int32, (tokens, pairs), 0), 1.0, 0.0))
        scatter = [dot(rounded(s), owner, CROSS) for s in scatter]
    copies[2].wait()
    packed = dot(rounded(scatter[0]), acts[...])
    copies[3].wait()
    packed = rounded(packed + dot(rounded(scatter[1]), cot[...]))
    tiles = blocks[0].shape[0]
    for k, block in enumerate(blocks):
        for i in range(tiles):
            at = (k * tiles + i) * TILE
            block[i] = packed[at : at + TILE]
    copies[1].wait()
    weight = jnp.broadcast_to(probs[...].astype(jnp.float32), (pairs, pairs))
    weight = jnp.sum(jnp.where(p == q, weight, 0.0), axis=1, keepdims=True)
    slot = lax.broadcasted_iota(jnp.int32, (pairs, LANES), 1)
    for t in range(2):
        mix = jnp.where(slot == col_slot + t * cap, weight, 0.0)
        mix_out[t] = mix if owner is None else dot(owner, rounded(mix))


def fill(rows, at, ins, first, deep, tiles):
    spots = [(ref, b + first + i) for ref in ins for b in range(0, ref.shape[0], tiles) for i in range(deep)]
    for i in range(0, len(spots), 2):
        pair = [ref[b] for ref, b in spots[i : i + 2]]
        rows[at + i * TILE : at + (i + 2) * TILE] = jnp.concatenate(pair, axis=0)


def near_kernel(cap, count, *refs):
    stored, ins, (acts, cot), held, sems = refs[:3], refs[3 : 3 + count], refs[3 + count : 5 + count], refs[5 + count : -1], refs[-1]
    copies = [pltpu.make_async_copy(s, h, sems.at[i]) for i, (s, h) in enumerate(zip(stored, held))]
    for copy in copies:
        copy.start()
    deep, tiles = -(-cap // TILE), 2 * cap // TILE
    fill(acts, 0, ins, 0, deep, tiles)
    fill(cot, 0, ins, tiles - deep, deep, tiles)
    for copy in copies:
        copy.wait()


def expert_kernel(cap, count, w_gate, w_up, w_down, acts_in, cot_in, *refs):
    ins, outs, (acts, cot) = refs[:count], refs[count : 3 * count], refs[3 * count :]
    width = acts.shape[1]
    tiles = 2 * cap // TILE
    deep = -(-cap // TILE)
    lead = deep * TILE - cap
    places = [(out, b) for out in outs for b in range(0, out.shape[0], tiles)]
    tall = len(places) * deep * TILE
    near = count * deep * TILE
    fill(acts, near, ins, 0, deep, tiles)
    fill(cot, near, ins, tiles - deep, deep, tiles)
    grad_hidden = dot(w_down[...], cot[...], CROSS).T
    gate_pre = dot(acts[...], w_gate[...])
    up_pre = dot(acts[...], w_up[...])
    if lead:
        grad_hidden = pltpu.roll(grad_hidden, tall - lead, 0)
    live = lax.broadcasted_iota(jnp.int32, gate_pre.shape, 0) % (deep * TILE) < cap
    squash = jax.nn.sigmoid(gate_pre)
    silu = gate_pre * squash
    hidden = rounded(jnp.where(live, silu * up_pre, 0.0))
    grad_gate = jnp.where(live, grad_hidden * up_pre * squash * (1.0 + gate_pre * (1.0 - squash)), 0.0)
    grad_up = jnp.where(live, grad_hidden * silu, 0.0)
    if lead:
        grad_gate, grad_up = pltpu.roll(grad_gate, lead, 0), pltpu.roll(grad_up, lead, 0)
    grad_gate, grad_up = rounded(grad_gate), rounded(grad_up)
    step = width // 2
    for at in range(0, width, step):
        cols = slice(at, at + step)
        out = dot(hidden, w_down[:, cols])
        grad = dot(w_gate[cols, :], grad_gate, CROSS) + dot(w_up[cols, :], grad_up, CROSS)
        grad = rounded(grad).T.astype(jnp.float32)
        for n, (ref, b) in enumerate(places):
            base = n * deep * TILE
            for i in range(tiles):
                parts = []
                if i < deep:
                    parts.append(out[base + i * TILE : base + (i + 1) * TILE])
                if i >= tiles - deep:
                    j = i - (tiles - deep)
                    parts.append(grad[base + j * TILE : base + (j + 1) * TILE])
                ref[b + i, :, cols] = rounded(sum(parts))


def sum_kernel(*refs):
    total = refs[0][...].astype(jnp.float32)
    for ref in refs[1:-1]:
        total = total + ref[...].astype(jnp.float32)
    refs[-1][...] = rounded(total)


def finish_kernel(which, cap, count, keep, mix, base, *refs):
    own, back, result = refs[:count], refs[count:-1], refs[-1]
    tiles, deep = 2 * cap // TILE, -(-cap // TILE)
    mixed = jnp.zeros(base.shape, jnp.float32)
    weights = rounded(mix[which])
    for i in range(deep) if which == 0 else range(tiles - deep, tiles):
        rows = own[0][i].astype(jnp.float32)
        for ref in own[1:]:
            rows = rows + ref[i].astype(jnp.float32)
        for k, rows in enumerate([rounded(rows)] + [ref[i] for ref in back]):
            at = (k * tiles + i) * TILE
            mixed = mixed + dot(weights[:, at : at + TILE], rows)
    result[...] = rounded(base[...].astype(jnp.float32) + keep[0, 0].astype(jnp.float32) * mixed)


def shards(acts, cotangent, routes, probs, keep, w_gate, w_up, w_down):
    experts = lax.axis_size("expert") // 2
    r = lax.axis_size("dp")
    token_count, width = acts.shape
    top = routes.shape[1]
    capacity = 2 * ((token_count * top * 5 + 8 * experts - 1) // (8 * experts))
    pairs = token_count * top
    tiles = 2 * capacity // TILE
    hidden = w_gate.shape[-1]
    shape = jax.ShapeDtypeStruct
    block = pltpu.VMEM((tiles, TILE, width), jnp.bfloat16)
    rest = pltpu.VMEM(((experts - 1) * tiles, TILE, width), jnp.bfloat16)
    far_off, vmem = pl.BlockSpec(memory_space=pltpu.HBM), pl.BlockSpec(memory_space=pltpu.VMEM)
    inputs = (routes.reshape(1, pairs), probs.reshape(1, pairs), acts, cotangent)
    mix, *sent = pl.pallas_call(
        functools.partial(pack_kernel, experts, capacity, top),
        in_specs=[far_off] * 4,
        out_specs=[vmem] * (1 + experts),
        out_shape=[pltpu.VMEM((2, token_count, LANES), jnp.float32)] + [block] * experts,
        scratch_shapes=[pltpu.VMEM(x.shape, x.dtype) for x in inputs] + [pltpu.SemaphoreType.DMA((4,))],
        compiler_params=room(4),
        name="pack",
    )(*map(in_hbm, inputs))

    members = [(half, by) for half in range(2) for by in range(r)]
    near = [sent[0]]
    got = [to_expert(sent[k], k) for k in range(1, experts)]
    near += [to_member(sent[0], half, by) for half, by in members[1:]]
    got = got[0] if experts == 2 else jnp.concatenate(got, axis=0)
    far = [got] + [to_member(got, half, by) for half, by in members[1:]]
    weights = (w_gate.reshape(width, hidden), w_up.reshape(width, hidden), w_down.reshape(hidden, width))
    tall = experts * 2 * r * (-(-capacity // TILE)) * TILE
    count = len(members)
    laid = pltpu.VMEM((tall, width), jnp.bfloat16)
    acts_rows, cot_rows, *held = pl.pallas_call(
        functools.partial(near_kernel, capacity, count),
        in_specs=[far_off] * 3 + [vmem] * count,
        out_specs=[vmem] * 5,
        out_shape=[laid] * 2 + [pltpu.VMEM(w.shape, w.dtype) for w in weights],
        scratch_shapes=[pltpu.SemaphoreType.DMA((3,))],
        compiler_params=room(4),
        name="near",
    )(*map(in_hbm, weights), *map(near_core, near))
    *parts, _, _ = pl.pallas_call(
        functools.partial(expert_kernel, capacity, count),
        in_specs=[vmem] * (5 + count),
        out_specs=[vmem] * (2 * count + 2),
        out_shape=[block] * count + [rest] * count + [laid] * 2,
        input_output_aliases={3: 2 * count, 4: 2 * count + 1},
        compiler_params=room(8),
        name="expert",
    )(*map(near_core, (*held, acts_rows, cot_rows, *far)))
    near, far = parts[:count], parts[count:]
    order = range(count - 1, 0, -1)
    far = [far[0]] + [to_member(far[i], members[i][0], -members[i][1]) for i in order]
    near = [near[0]] + [to_member(near[i], members[i][0], -members[i][1]) for i in order]
    total = pl.pallas_call(sum_kernel, out_shape=rest, compiler_params=room(4), name="total")(*map(near_core, far))
    back = [to_expert(total[(k - 1) * tiles : k * tiles], -k) for k in range(1, experts)]
    layer_out, section_grad = [
        pl.pallas_call(
            functools.partial(finish_kernel, which, capacity, count),
            in_specs=[pl.BlockSpec(memory_space=pltpu.SMEM)] + [vmem] * (2 + count + len(back)),
            out_shape=shape(acts.shape, jnp.bfloat16) if which == 0 else pltpu.VMEM(acts.shape, jnp.bfloat16),
            compiler_params=room(4),
            name=name,
        )(keep, *map(near_core, (mix, base, *near, *back)))
        for which, name, base in ((0, "out", acts), (1, "grad", cotangent))
    ]
    return layer_out, to_below(section_grad)


def solution(mesh):
    rows = P(("pipe", "expert", "dp"), None)
    return jax.shard_map(
        shards,
        mesh=mesh,
        in_specs=(
            rows,
            rows,
            rows,
            rows,
            P("pipe", ("expert", "dp")),
            P("pipe", "expert", None, "dp"),
            P("pipe", "expert", None, "dp"),
            P("pipe", "expert", "dp", None),
        ),
        out_specs=(rows, rows),
        check_vma=False,
    )
```

```python
import functools

import jax
import jax.numpy as jnp
from jax import lax
from jax.experimental import pallas as pl
from jax.experimental.pallas import tpu as pltpu
from jax.sharding import PartitionSpec as P

CROSS = (((1,), (1,)), ((), ()))
LANES = 128
TILE = 4
MIB = 1024 * 1024


def room(mib):
    return pltpu.CompilerParams(vmem_limit_bytes=mib * MIB)


def rounded(x):
    return x.astype(jnp.bfloat16)


def in_hbm(x):
    return pltpu.with_memory_space_constraint(x, pltpu.HBM)


def near_core(x):
    return pltpu.with_memory_space_constraint(x, pltpu.VMEM)


def dot(a, b, dims=(((1,), (0,)), ((), ()))):
    return lax.dot_general(a, b, dims, preferred_element_type=jnp.float32)


def to_member(shard, half, by):
    n, r = lax.axis_size("expert"), lax.axis_size("dp")
    pairs = [(e * r + d, (e ^ half) * r + (d + by) % r) for e in range(n) for d in range(r)]
    return lax.ppermute(shard, ("expert", "dp"), pairs)


def to_expert(shard, by):
    n = lax.axis_size("expert")
    return lax.ppermute(shard, "expert", [(e, (e + 2 * by) % n) for e in range(n)])


def to_below(shard):
    return lax.ppermute(shard, "pipe", [(p, p - 1) for p in range(1, lax.axis_size("pipe"))])


def pack_kernel(experts, cap, top, *refs):
    stored, mix_out, blocks = refs[:4], refs[4], refs[5 : 5 + experts]
    held, sems = refs[5 + experts : -1], refs[-1]
    copies = [pltpu.make_async_copy(s, h, sems.at[i]) for i, (s, h) in enumerate(zip(stored, held))]
    for copy in copies:
        copy.start()
    routes, probs, acts, cot = held
    pairs = routes.shape[1]
    tokens = pairs // top
    copies[0].wait()
    chosen = jnp.broadcast_to(routes[...], (pairs, pairs))
    p = lax.broadcasted_iota(jnp.int32, (pairs, pairs), 0)
    q = lax.broadcasted_iota(jnp.int32, (pairs, pairs), 1)
    column = jnp.sum(jnp.where(p == q, chosen, 0), axis=1, keepdims=True)
    alike = column == chosen
    mine = lax.axis_index("expert") // 2

    def slot_of(expert, rank):
        far = expert - mine
        return jnp.where(far < 0, far + experts, far) * (2 * cap) + rank

    row_slot = slot_of(routes[...], jnp.sum(jnp.where(alike & (p < q), 1, 0), axis=0, keepdims=True))
    col_slot = slot_of(column, jnp.sum(jnp.where(alike & (q < p), 1, 0), axis=1, keepdims=True))
    slot = lax.broadcasted_iota(jnp.int32, (2 * experts * cap, pairs), 0)
    scatter = [jnp.where(slot == row_slot + t * cap, 1.0, 0.0) for t in range(2)]
    owner = None
    if top > 1:
        owner = lax.broadcasted_iota(jnp.int32, (tokens, pairs), 1) // top
        owner = rounded(jnp.where(owner == lax.broadcasted_iota(jnp.int32, (tokens, pairs), 0), 1.0, 0.0))
        scatter = [dot(rounded(s), owner, CROSS) for s in scatter]
    copies[2].wait()
    packed = dot(rounded(scatter[0]), acts[...])
    copies[3].wait()
    packed = rounded(packed + dot(rounded(scatter[1]), cot[...]))
    tiles = blocks[0].shape[0]
    for k, block in enumerate(blocks):
        for i in range(tiles):
            at = (k * tiles + i) * TILE
            block[i] = packed[at : at + TILE]
    copies[1].wait()
    weight = jnp.broadcast_to(probs[...].astype(jnp.float32), (pairs, pairs))
    weight = jnp.sum(jnp.where(p == q, weight, 0.0), axis=1, keepdims=True)
    slot = lax.broadcasted_iota(jnp.int32, (pairs, LANES), 1)
    for t in range(2):
        mix = jnp.where(slot == col_slot + t * cap, weight, 0.0)
        mix_out[t] = mix if owner is None else dot(owner, rounded(mix))


def fill(rows, at, ins, first, deep, tiles):
    spots = [(ref, b + first + i) for ref in ins for b in range(0, ref.shape[0], tiles) for i in range(deep)]
    for i in range(0, len(spots), 2):
        pair = [ref[b] for ref, b in spots[i : i + 2]]
        rows[at + i * TILE : at + (i + 2) * TILE] = jnp.concatenate(pair, axis=0)


def near_kernel(cap, count, *refs):
    stored, ins, (acts, cot), held, sems = refs[:3], refs[3 : 3 + count], refs[3 + count : 5 + count], refs[5 + count : -1], refs[-1]
    copies = [pltpu.make_async_copy(s, h, sems.at[i]) for i, (s, h) in enumerate(zip(stored, held))]
    for copy in copies:
        copy.start()
    deep, tiles = -(-cap // TILE), 2 * cap // TILE
    fill(acts, 0, ins, 0, deep, tiles)
    fill(cot, 0, ins, tiles - deep, deep, tiles)
    for copy in copies:
        copy.wait()


def expert_kernel(cap, count, w_gate, w_up, w_down, acts_in, cot_in, *refs):
    ins, outs, (acts, cot) = (refs[0], *refs[count - 1 : 0 : -1]), refs[count : 3 * count], refs[3 * count :]
    width = acts.shape[1]
    tiles = 2 * cap // TILE
    deep = -(-cap // TILE)
    lead = deep * TILE - cap
    places = [(out, b) for out in outs for b in range(0, out.shape[0], tiles)]
    tall = len(places) * deep * TILE
    near = count * deep * TILE
    fill(acts, near, ins, 0, deep, tiles)
    fill(cot, near, ins, tiles - deep, deep, tiles)
    grad_hidden = dot(w_down[...], cot[...], CROSS).T
    gate_pre = dot(acts[...], w_gate[...])
    up_pre = dot(acts[...], w_up[...])
    if lead:
        grad_hidden = pltpu.roll(grad_hidden, tall - lead, 0)
    live = lax.broadcasted_iota(jnp.int32, gate_pre.shape, 0) % (deep * TILE) < cap
    squash = jax.nn.sigmoid(gate_pre)
    silu = gate_pre * squash
    hidden = rounded(jnp.where(live, silu * up_pre, 0.0))
    grad_gate = jnp.where(live, grad_hidden * up_pre * squash * (1.0 + gate_pre * (1.0 - squash)), 0.0)
    grad_up = jnp.where(live, grad_hidden * silu, 0.0)
    if lead:
        grad_gate, grad_up = pltpu.roll(grad_gate, lead, 0), pltpu.roll(grad_up, lead, 0)
    grad_gate, grad_up = rounded(grad_gate), rounded(grad_up)
    step = width // 2
    for at in range(0, width, step):
        cols = slice(at, at + step)
        out = dot(hidden, w_down[:, cols])
        grad = dot(w_gate[cols, :], grad_gate, CROSS) + dot(w_up[cols, :], grad_up, CROSS)
        grad = rounded(grad).T.astype(jnp.float32)
        for n, (ref, b) in enumerate(places):
            base = n * deep * TILE
            for i in range(tiles):
                parts = []
                if i < deep:
                    parts.append(out[base + i * TILE : base + (i + 1) * TILE])
                if i >= tiles - deep:
                    j = i - (tiles - deep)
                    parts.append(grad[base + j * TILE : base + (j + 1) * TILE])
                ref[b + i, :, cols] = rounded(sum(parts))


def sum_kernel(*refs):
    total = refs[0][...].astype(jnp.float32)
    for ref in refs[1:-1]:
        total = total + ref[...].astype(jnp.float32)
    refs[-1][...] = rounded(total)


def finish_kernel(which, cap, count, keep, mix, base, *refs):
    own, back, result = refs[:count], refs[count:-1], refs[-1]
    tiles, deep = 2 * cap // TILE, -(-cap // TILE)
    mixed = jnp.zeros(base.shape, jnp.float32)
    weights = rounded(mix[which])
    for i in range(deep) if which == 0 else range(tiles - deep, tiles):
        rows = own[0][i].astype(jnp.float32)
        for ref in own[1:]:
            rows = rows + ref[i].astype(jnp.float32)
        for k, rows in enumerate([rounded(rows)] + [ref[i] for ref in back]):
            at = (k * tiles + i) * TILE
            mixed = mixed + dot(weights[:, at : at + TILE], rows)
    result[...] = rounded(base[...].astype(jnp.float32) + keep[0, 0].astype(jnp.float32) * mixed)


def shards(acts, cotangent, routes, probs, keep, w_gate, w_up, w_down):
    experts = lax.axis_size("expert") // 2
    r = lax.axis_size("dp")
    token_count, width = acts.shape
    top = routes.shape[1]
    capacity = 2 * ((token_count * top * 5 + 8 * experts - 1) // (8 * experts))
    pairs = token_count * top
    tiles = 2 * capacity // TILE
    hidden = w_gate.shape[-1]
    shape = jax.ShapeDtypeStruct
    block = pltpu.VMEM((tiles, TILE, width), jnp.bfloat16)
    rest = pltpu.VMEM(((experts - 1) * tiles, TILE, width), jnp.bfloat16)
    far_off, vmem = pl.BlockSpec(memory_space=pltpu.HBM), pl.BlockSpec(memory_space=pltpu.VMEM)
    inputs = (routes.reshape(1, pairs), probs.reshape(1, pairs), acts, cotangent)
    mix, *sent = pl.pallas_call(
        functools.partial(pack_kernel, experts, capacity, top),
        in_specs=[far_off] * 4,
        out_specs=[vmem] * (1 + experts),
        out_shape=[pltpu.VMEM((2, token_count, LANES), jnp.float32)] + [block] * experts,
        scratch_shapes=[pltpu.VMEM(x.shape, x.dtype) for x in inputs] + [pltpu.SemaphoreType.DMA((4,))],
        compiler_params=room(4),
        name="pack",
    )(*map(in_hbm, inputs))

    members = [(half, by) for half in range(2) for by in range(r)]
    near = [sent[0]]
    got = [to_expert(sent[k], k) for k in range(1, experts)]
    near += [to_member(sent[0], half, by) for half, by in members[1:]]
    got = got[0] if experts == 2 else jnp.concatenate(got, axis=0)
    far = [got] + [to_member(got, half, by) for half, by in members[1:]]
    weights = (w_gate.reshape(width, hidden), w_up.reshape(width, hidden), w_down.reshape(hidden, width))
    tall = experts * 2 * r * (-(-capacity // TILE)) * TILE
    count = len(members)
    laid = pltpu.VMEM((tall, width), jnp.bfloat16)
    acts_rows, cot_rows, *held = pl.pallas_call(
        functools.partial(near_kernel, capacity, count),
        in_specs=[far_off] * 3 + [vmem] * count,
        out_specs=[vmem] * 5,
        out_shape=[laid] * 2 + [pltpu.VMEM(w.shape, w.dtype) for w in weights],
        scratch_shapes=[pltpu.SemaphoreType.DMA((3,))],
        compiler_params=room(4),
        name="near",
    )(*map(in_hbm, weights), *map(near_core, near))
    *parts, _, _ = pl.pallas_call(
        functools.partial(expert_kernel, capacity, count),
        in_specs=[vmem] * (5 + count),
        out_specs=[vmem] * (2 * count + 2),
        out_shape=[block] * count + [rest] * count + [laid] * 2,
        input_output_aliases={3: 2 * count, 4: 2 * count + 1},
        compiler_params=room(8),
        name="expert",
    )(*map(near_core, (*held, acts_rows, cot_rows, far[0], *far[:0:-1])))
    near, far = parts[:count], parts[count:]
    far = [far[0]] + [to_member(x, half, -by) for x, (half, by) in zip(far[:0:-1], members[:0:-1])]
    near = [near[0]] + [to_member(x, half, -by) for x, (half, by) in zip(near[1:], members[1:])]
    total = pl.pallas_call(sum_kernel, out_shape=rest, compiler_params=room(4), name="total")(*map(near_core, far))
    back = [to_expert(total[(k - 1) * tiles : k * tiles], -k) for k in range(1, experts)]
    layer_out, section_grad = [
        pl.pallas_call(
            functools.partial(finish_kernel, which, capacity, count),
            in_specs=[pl.BlockSpec(memory_space=pltpu.SMEM)] + [vmem] * (2 + count + len(back)),
            out_shape=shape(acts.shape, jnp.bfloat16) if which == 0 else pltpu.VMEM(acts.shape, jnp.bfloat16),
            compiler_params=room(4),
            name=name,
        )(keep, *map(near_core, (mix, base, *near, *back)))
        for which, name, base in ((0, "out", acts), (1, "grad", cotangent))
    ]
    return layer_out, to_below(section_grad)


def solution(mesh):
    rows = P(("pipe", "expert", "dp"), None)
    return jax.shard_map(
        shards,
        mesh=mesh,
        in_specs=(
            rows,
            rows,
            rows,
            rows,
            P("pipe", ("expert", "dp")),
            P("pipe", "expert", None, "dp"),
            P("pipe", "expert", None, "dp"),
            P("pipe", "expert", "dp", None),
        ),
        out_specs=(rows, rows),
        check_vma=False,
    )
```

```python
import functools

import jax
import jax.numpy as jnp
from jax import lax
from jax.experimental import pallas as pl
from jax.experimental.pallas import tpu as pltpu
from jax.sharding import PartitionSpec as P

CROSS = (((1,), (1,)), ((), ()))
LANES = 128
TILE = 4
SPLIT = 1
MIB = 1024 * 1024


def room(mib):
    return pltpu.CompilerParams(vmem_limit_bytes=mib * MIB)


def rounded(x):
    return x.astype(jnp.bfloat16)


def in_hbm(x):
    return pltpu.with_memory_space_constraint(x, pltpu.HBM)


def near_core(x):
    return pltpu.with_memory_space_constraint(x, pltpu.VMEM)


def dot(a, b, dims=(((1,), (0,)), ((), ()))):
    return lax.dot_general(a, b, dims, preferred_element_type=jnp.float32)


def to_member(shard, half, by):
    n, r = lax.axis_size("expert"), lax.axis_size("dp")
    pairs = [(e * r + d, (e ^ half) * r + (d + by) % r) for e in range(n) for d in range(r)]
    return lax.ppermute(shard, ("expert", "dp"), pairs)


def to_expert(shard, by):
    n = lax.axis_size("expert")
    return lax.ppermute(shard, "expert", [(e, (e + 2 * by) % n) for e in range(n)])


def to_below(shard):
    return lax.ppermute(shard, "pipe", [(p, p - 1) for p in range(1, lax.axis_size("pipe"))])


def pack_kernel(experts, cap, top, *refs):
    stored, mix_out, blocks = refs[:4], refs[4], refs[5 : 5 + experts]
    held, sems = refs[5 + experts : -1], refs[-1]
    copies = [pltpu.make_async_copy(s, h, sems.at[i]) for i, (s, h) in enumerate(zip(stored, held))]
    for copy in copies:
        copy.start()
    routes, probs, acts, cot = held
    pairs = routes.shape[1]
    tokens = pairs // top
    copies[0].wait()
    chosen = jnp.broadcast_to(routes[...], (pairs, pairs))
    p = lax.broadcasted_iota(jnp.int32, (pairs, pairs), 0)
    q = lax.broadcasted_iota(jnp.int32, (pairs, pairs), 1)
    column = jnp.sum(jnp.where(p == q, chosen, 0), axis=1, keepdims=True)
    alike = column == chosen
    mine = lax.axis_index("expert") // 2

    def slot_of(expert, rank):
        far = expert - mine
        return jnp.where(far < 0, far + experts, far) * (2 * cap) + rank

    row_slot = slot_of(routes[...], jnp.sum(jnp.where(alike & (p < q), 1, 0), axis=0, keepdims=True))
    col_slot = slot_of(column, jnp.sum(jnp.where(alike & (q < p), 1, 0), axis=1, keepdims=True))
    slot = lax.broadcasted_iota(jnp.int32, (2 * experts * cap, pairs), 0)
    scatter = [jnp.where(slot == row_slot + t * cap, 1.0, 0.0) for t in range(2)]
    owner = None
    if top > 1:
        owner = lax.broadcasted_iota(jnp.int32, (tokens, pairs), 1) // top
        owner = rounded(jnp.where(owner == lax.broadcasted_iota(jnp.int32, (tokens, pairs), 0), 1.0, 0.0))
        scatter = [dot(rounded(s), owner, CROSS) for s in scatter]
    copies[2].wait()
    packed = dot(rounded(scatter[0]), acts[...])
    copies[3].wait()
    packed = rounded(packed + dot(rounded(scatter[1]), cot[...]))
    tiles = blocks[0].shape[0]
    for k, block in enumerate(blocks):
        for i in range(tiles):
            at = (k * tiles + i) * TILE
            block[i] = packed[at : at + TILE]
    copies[1].wait()
    weight = jnp.broadcast_to(probs[...].astype(jnp.float32), (pairs, pairs))
    weight = jnp.sum(jnp.where(p == q, weight, 0.0), axis=1, keepdims=True)
    slot = lax.broadcasted_iota(jnp.int32, (pairs, LANES), 1)
    for t in range(2):
        mix = jnp.where(slot == col_slot + t * cap, weight, 0.0)
        mix_out[t] = mix if owner is None else dot(owner, rounded(mix))


def fill(rows, at, ins, first, deep, tiles):
    spots = [(ref, b + first + i) for ref in ins for b in range(0, ref.shape[0], tiles) for i in range(deep)]
    while spots:
        take = 2 if at % (2 * TILE) == 0 and len(spots) > 1 else 1
        some = [ref[b] for ref, b in spots[:take]]
        rows[at : at + take * TILE] = jnp.concatenate(some, axis=0) if take > 1 else some[0]
        at, spots = at + take * TILE, spots[take:]


def near_kernel(cap, count, split, *refs):
    stored, ins, (acts, cot), held, sems = refs[:3], refs[3 : 3 + count], refs[3 + count : 5 + count], refs[5 + count : -1], refs[-1]
    copies = []
    for store, hold in zip(stored, held):
        part = store.shape[0] // split
        for i in range(split):
            span = pl.ds(i * part, part)
            copies.append(pltpu.make_async_copy(store.at[span], hold.at[span], sems.at[len(copies)]))
            copies[-1].start()
    deep, tiles = -(-cap // TILE), 2 * cap // TILE
    fill(acts, 0, ins, 0, deep, tiles)
    fill(cot, 0, ins, tiles - deep, deep, tiles)
    for copy in copies:
        copy.wait()


def expert_kernel(cap, count, w_gate, w_up, w_down, acts_in, cot_in, *refs):
    late, *ins = refs[: count + 1]
    ins, outs, (acts, cot) = [ins[0], *ins[:0:-1]], refs[count + 1 : 3 * count + 1], refs[3 * count + 1 :]
    width = acts.shape[1]
    tiles = 2 * cap // TILE
    deep = -(-cap // TILE)
    lead = deep * TILE - cap
    places = [(out, b) for out in outs for b in range(0, out.shape[0], tiles)]
    tall = len(places) * deep * TILE
    near = count * deep * TILE
    near -= deep * TILE
    fill(acts, near, [late, *ins], 0, deep, tiles)
    fill(cot, near, [late, *ins], tiles - deep, deep, tiles)
    grad_hidden = dot(w_down[...], cot[...], CROSS).T
    gate_pre = dot(acts[...], w_gate[...])
    up_pre = dot(acts[...], w_up[...])
    if lead:
        grad_hidden = pltpu.roll(grad_hidden, tall - lead, 0)
    live = lax.broadcasted_iota(jnp.int32, gate_pre.shape, 0) % (deep * TILE) < cap
    squash = jax.nn.sigmoid(gate_pre)
    silu = gate_pre * squash
    hidden = rounded(jnp.where(live, silu * up_pre, 0.0))
    grad_gate = jnp.where(live, grad_hidden * up_pre * squash * (1.0 + gate_pre * (1.0 - squash)), 0.0)
    grad_up = jnp.where(live, grad_hidden * silu, 0.0)
    if lead:
        grad_gate, grad_up = pltpu.roll(grad_gate, lead, 0), pltpu.roll(grad_up, lead, 0)
    grad_gate, grad_up = rounded(grad_gate), rounded(grad_up)
    step = width // 2
    for at in range(0, width, step):
        cols = slice(at, at + step)
        out = dot(hidden, w_down[:, cols])
        grad = dot(w_gate[cols, :], grad_gate, CROSS) + dot(w_up[cols, :], grad_up, CROSS)
        grad = rounded(grad).T.astype(jnp.float32)
        for n, (ref, b) in enumerate(places):
            base = n * deep * TILE
            for i in range(tiles):
                parts = []
                if i < deep:
                    parts.append(out[base + i * TILE : base + (i + 1) * TILE])
                if i >= tiles - deep:
                    j = i - (tiles - deep)
                    parts.append(grad[base + j * TILE : base + (j + 1) * TILE])
                ref[b + i, :, cols] = rounded(sum(parts))


def sum_kernel(*refs):
    total = refs[0][...].astype(jnp.float32)
    for ref in refs[1:-1]:
        total = total + ref[...].astype(jnp.float32)
    refs[-1][...] = rounded(total)


def finish_kernel(which, cap, count, keep, mix, base, *refs):
    own, back, result = refs[:count], refs[count:-1], refs[-1]
    tiles, deep = 2 * cap // TILE, -(-cap // TILE)
    mixed = jnp.zeros(base.shape, jnp.float32)
    weights = rounded(mix[which])
    for i in range(deep) if which == 0 else range(tiles - deep, tiles):
        rows = own[0][i].astype(jnp.float32)
        for ref in own[1:]:
            rows = rows + ref[i].astype(jnp.float32)
        for k, rows in enumerate([rounded(rows)] + [ref[i] for ref in back]):
            at = (k * tiles + i) * TILE
            mixed = mixed + dot(weights[:, at : at + TILE], rows)
    result[...] = rounded(base[...].astype(jnp.float32) + keep[0, 0].astype(jnp.float32) * mixed)


def shards(acts, cotangent, routes, probs, keep, w_gate, w_up, w_down):
    experts = lax.axis_size("expert") // 2
    r = lax.axis_size("dp")
    token_count, width = acts.shape
    top = routes.shape[1]
    capacity = 2 * ((token_count * top * 5 + 8 * experts - 1) // (8 * experts))
    pairs = token_count * top
    tiles = 2 * capacity // TILE
    hidden = w_gate.shape[-1]
    shape = jax.ShapeDtypeStruct
    block = pltpu.VMEM((tiles, TILE, width), jnp.bfloat16)
    rest = pltpu.VMEM(((experts - 1) * tiles, TILE, width), jnp.bfloat16)
    far_off, vmem = pl.BlockSpec(memory_space=pltpu.HBM), pl.BlockSpec(memory_space=pltpu.VMEM)
    inputs = (routes.reshape(1, pairs), probs.reshape(1, pairs), acts, cotangent)
    mix, *sent = pl.pallas_call(
        functools.partial(pack_kernel, experts, capacity, top),
        in_specs=[far_off] * 4,
        out_specs=[vmem] * (1 + experts),
        out_shape=[pltpu.VMEM((2, token_count, LANES), jnp.float32)] + [block] * experts,
        scratch_shapes=[pltpu.VMEM(x.shape, x.dtype) for x in inputs] + [pltpu.SemaphoreType.DMA((4,))],
        compiler_params=room(4),
        name="pack",
    )(*map(in_hbm, inputs))

    members = [(half, by) for half in range(2) for by in range(r)]
    near = [sent[0]]
    got = [to_expert(sent[k], k) for k in range(1, experts)]
    near += [to_member(sent[0], half, by) for half, by in members[1:]]
    got = got[0] if experts == 2 else jnp.concatenate(got, axis=0)
    far = [got] + [to_member(got, half, by) for half, by in members[1:]]
    weights = (w_gate.reshape(width, hidden), w_up.reshape(width, hidden), w_down.reshape(hidden, width))
    tall = experts * 2 * r * (-(-capacity // TILE)) * TILE
    count = len(members)
    laid = pltpu.VMEM((tall, width), jnp.bfloat16)
    acts_rows, cot_rows, *held = pl.pallas_call(
        functools.partial(near_kernel, capacity, count - 1, SPLIT),
        in_specs=[far_off] * 3 + [vmem] * (count - 1),
        out_specs=[vmem] * 5,
        out_shape=[laid] * 2 + [pltpu.VMEM(w.shape, w.dtype) for w in weights],
        scratch_shapes=[pltpu.SemaphoreType.DMA((3 * SPLIT,))],
        compiler_params=room(4),
        name="near",
    )(*map(in_hbm, weights), *map(near_core, near[:-1]))
    *parts, _, _ = pl.pallas_call(
        functools.partial(expert_kernel, capacity, count),
        in_specs=[vmem] * (6 + count),
        out_specs=[vmem] * (2 * count + 2),
        out_shape=[block] * count + [rest] * count + [laid] * 2,
        input_output_aliases={3: 2 * count, 4: 2 * count + 1},
        compiler_params=room(8),
        name="expert",
    )(*map(near_core, (*held, acts_rows, cot_rows, near[-1], far[0], *far[:0:-1])))
    near, far = parts[:count], parts[count:]
    far = [far[0]] + [to_member(x, half, -by) for x, (half, by) in zip(far[:0:-1], members[:0:-1])]
    near = [near[0]] + [to_member(x, half, -by) for x, (half, by) in zip(near[1:], members[1:])]
    total = pl.pallas_call(sum_kernel, out_shape=rest, compiler_params=room(4), name="total")(*map(near_core, far))
    back = [to_expert(total[(k - 1) * tiles : k * tiles], -k) for k in range(1, experts)]
    layer_out, section_grad = [
        pl.pallas_call(
            functools.partial(finish_kernel, which, capacity, count),
            in_specs=[pl.BlockSpec(memory_space=pltpu.SMEM)] + [vmem] * (2 + count + len(back)),
            out_shape=shape(acts.shape, jnp.bfloat16) if which == 0 else pltpu.VMEM(acts.shape, jnp.bfloat16),
            compiler_params=room(4),
            name=name,
        )(keep, *map(near_core, (mix, base, *near, *back)))
        for which, name, base in ((0, "out", acts), (1, "grad", cotangent))
    ]
    return layer_out, to_below(section_grad)


def solution(mesh):
    rows = P(("pipe", "expert", "dp"), None)
    return jax.shard_map(
        shards,
        mesh=mesh,
        in_specs=(
            rows,
            rows,
            rows,
            rows,
            P("pipe", ("expert", "dp")),
            P("pipe", "expert", None, "dp"),
            P("pipe", "expert", None, "dp"),
            P("pipe", "expert", "dp", None),
        ),
        out_specs=(rows, rows),
        check_vma=False,
    )
```

```python
import functools

import jax
import jax.numpy as jnp
from jax import lax
from jax.experimental import pallas as pl
from jax.experimental.pallas import tpu as pltpu
from jax.sharding import PartitionSpec as P

CROSS = (((1,), (1,)), ((), ()))
LANES = 128
TILE = 4
MIB = 1024 * 1024


def room(mib):
    return pltpu.CompilerParams(vmem_limit_bytes=mib * MIB)


def rounded(x):
    return x.astype(jnp.bfloat16)


def in_hbm(x):
    return pltpu.with_memory_space_constraint(x, pltpu.HBM)


def near_core(x):
    return pltpu.with_memory_space_constraint(x, pltpu.VMEM)


def dot(a, b, dims=(((1,), (0,)), ((), ()))):
    return lax.dot_general(a, b, dims, preferred_element_type=jnp.float32)


def to_member(shard, half, by):
    n, r = lax.axis_size("expert"), lax.axis_size("dp")
    pairs = [(e * r + d, (e ^ half) * r + (d + by) % r) for e in range(n) for d in range(r)]
    return lax.ppermute(shard, ("expert", "dp"), pairs)


def to_expert(shard, by):
    n = lax.axis_size("expert")
    return lax.ppermute(shard, "expert", [(e, (e + 2 * by) % n) for e in range(n)])


def to_below(shard):
    return lax.ppermute(shard, "pipe", [(p, p - 1) for p in range(1, lax.axis_size("pipe"))])


def pack_kernel(experts, cap, top, *refs):
    stored, mix_out, blocks = refs[:4], refs[4], refs[5 : 5 + experts]
    held, sems = refs[5 + experts : -1], refs[-1]
    routes, probs, rows = held
    pairs = routes.shape[1]
    tokens = pairs // top
    places = (routes, probs, rows.at[:tokens], rows.at[tokens:])
    copies = [pltpu.make_async_copy(s, h, sems.at[i]) for i, (s, h) in enumerate(zip(stored, places))]
    for copy in copies:
        copy.start()
    copies[0].wait()
    chosen = jnp.broadcast_to(routes[...], (pairs, pairs))
    p = lax.broadcasted_iota(jnp.int32, (pairs, pairs), 0)
    q = lax.broadcasted_iota(jnp.int32, (pairs, pairs), 1)
    column = jnp.sum(jnp.where(p == q, chosen, 0), axis=1, keepdims=True)
    alike = column == chosen
    mine = lax.axis_index("expert") // 2

    def slot_of(expert, rank):
        far = expert - mine
        return jnp.where(far < 0, far + experts, far) * (2 * cap) + rank

    row_slot = slot_of(routes[...], jnp.sum(jnp.where(alike & (p < q), 1, 0), axis=0, keepdims=True))
    col_slot = slot_of(column, jnp.sum(jnp.where(alike & (q < p), 1, 0), axis=1, keepdims=True))
    slot = lax.broadcasted_iota(jnp.int32, (2 * experts * cap, pairs), 0)
    scatter = [jnp.where(slot == row_slot + t * cap, 1.0, 0.0) for t in range(2)]
    owner = None
    if top > 1:
        owner = lax.broadcasted_iota(jnp.int32, (tokens, pairs), 1) // top
        owner = rounded(jnp.where(owner == lax.broadcasted_iota(jnp.int32, (tokens, pairs), 0), 1.0, 0.0))
        scatter = [dot(rounded(s), owner, CROSS) for s in scatter]
    scatter = rounded(jnp.concatenate(scatter, axis=1))
    copies[2].wait()
    copies[3].wait()
    packed = rounded(dot(scatter, rows[...]))
    tiles = blocks[0].shape[0]
    for k, block in enumerate(blocks):
        for i in range(tiles):
            at = (k * tiles + i) * TILE
            block[i] = packed[at : at + TILE]
    copies[1].wait()
    weight = jnp.broadcast_to(probs[...].astype(jnp.float32), (pairs, pairs))
    weight = jnp.sum(jnp.where(p == q, weight, 0.0), axis=1, keepdims=True)
    slot = lax.broadcasted_iota(jnp.int32, (pairs, LANES), 1)
    for t in range(2):
        mix = jnp.where(slot == col_slot + t * cap, weight, 0.0)
        mix_out[t] = mix if owner is None else dot(owner, rounded(mix))


def fill(rows, at, ins, first, deep, tiles):
    spots = [(ref, b + first + i) for ref in ins for b in range(0, ref.shape[0], tiles) for i in range(deep)]
    for i in range(0, len(spots), 2):
        pair = [ref[b] for ref, b in spots[i : i + 2]]
        rows[at + i * TILE : at + (i + 2) * TILE] = jnp.concatenate(pair, axis=0)


def near_kernel(cap, count, *refs):
    stored, ins, (acts, cot), held, sems = refs[:3], refs[3 : 3 + count], refs[3 + count : 5 + count], refs[5 + count : -1], refs[-1]
    copies = [pltpu.make_async_copy(s, h, sems.at[i]) for i, (s, h) in enumerate(zip(stored, held))]
    for copy in copies:
        copy.start()
    deep, tiles = -(-cap // TILE), 2 * cap // TILE
    fill(acts, 0, ins, 0, deep, tiles)
    fill(cot, 0, ins, tiles - deep, deep, tiles)
    for copy in copies:
        copy.wait()


def expert_kernel(cap, count, w_gate, w_up, w_down, acts_in, cot_in, *refs):
    ins, outs, (acts, cot) = (refs[0], *refs[count - 1 : 0 : -1]), refs[count : 3 * count], refs[3 * count :]
    width = acts.shape[1]
    tiles = 2 * cap // TILE
    deep = -(-cap // TILE)
    lead = deep * TILE - cap
    places = [(out, b) for out in outs for b in range(0, out.shape[0], tiles)]
    tall = len(places) * deep * TILE
    near = count * deep * TILE
    fill(acts, near, ins, 0, deep, tiles)
    fill(cot, near, ins, tiles - deep, deep, tiles)
    grad_hidden = dot(w_down[...], cot[...], CROSS).T
    gate_pre = dot(acts[...], w_gate[...])
    up_pre = dot(acts[...], w_up[...])
    if lead:
        grad_hidden = pltpu.roll(grad_hidden, tall - lead, 0)
    live = lax.broadcasted_iota(jnp.int32, gate_pre.shape, 0) % (deep * TILE) < cap
    squash = jax.nn.sigmoid(gate_pre)
    silu = gate_pre * squash
    hidden = rounded(jnp.where(live, silu * up_pre, 0.0))
    grad_gate = jnp.where(live, grad_hidden * up_pre * squash * (1.0 + gate_pre * (1.0 - squash)), 0.0)
    grad_up = jnp.where(live, grad_hidden * silu, 0.0)
    if lead:
        grad_gate, grad_up = pltpu.roll(grad_gate, lead, 0), pltpu.roll(grad_up, lead, 0)
    grad_gate, grad_up = rounded(grad_gate), rounded(grad_up)
    step = width // 2
    for at in range(0, width, step):
        cols = slice(at, at + step)
        out = dot(hidden, w_down[:, cols])
        grad = dot(w_gate[cols, :], grad_gate, CROSS) + dot(w_up[cols, :], grad_up, CROSS)
        grad = rounded(grad).T.astype(jnp.float32)
        for n, (ref, b) in enumerate(places):
            base = n * deep * TILE
            for i in range(tiles):
                parts = []
                if i < deep:
                    parts.append(out[base + i * TILE : base + (i + 1) * TILE])
                if i >= tiles - deep:
                    j = i - (tiles - deep)
                    parts.append(grad[base + j * TILE : base + (j + 1) * TILE])
                ref[b + i, :, cols] = rounded(sum(parts))


def sum_kernel(*refs):
    total = refs[0][...].astype(jnp.float32)
    for ref in refs[1:-1]:
        total = total + ref[...].astype(jnp.float32)
    refs[-1][...] = rounded(total)


def finish_kernel(which, cap, count, keep, mix, base, *refs):
    own, back, result = refs[:count], refs[count:-1], refs[-1]
    tiles, deep = 2 * cap // TILE, -(-cap // TILE)
    mixed = jnp.zeros(base.shape, jnp.float32)
    weights = rounded(mix[which])
    for i in range(deep) if which == 0 else range(tiles - deep, tiles):
        rows = own[0][i].astype(jnp.float32)
        for ref in own[1:]:
            rows = rows + ref[i].astype(jnp.float32)
        for k, rows in enumerate([rounded(rows)] + [ref[i] for ref in back]):
            at = (k * tiles + i) * TILE
            mixed = mixed + dot(weights[:, at : at + TILE], rows)
    result[...] = rounded(base[...].astype(jnp.float32) + keep[0, 0].astype(jnp.float32) * mixed)


def shards(acts, cotangent, routes, probs, keep, w_gate, w_up, w_down):
    experts = lax.axis_size("expert") // 2
    r = lax.axis_size("dp")
    token_count, width = acts.shape
    top = routes.shape[1]
    capacity = 2 * ((token_count * top * 5 + 8 * experts - 1) // (8 * experts))
    pairs = token_count * top
    tiles = 2 * capacity // TILE
    hidden = w_gate.shape[-1]
    shape = jax.ShapeDtypeStruct
    block = pltpu.VMEM((tiles, TILE, width), jnp.bfloat16)
    rest = pltpu.VMEM(((experts - 1) * tiles, TILE, width), jnp.bfloat16)
    far_off, vmem = pl.BlockSpec(memory_space=pltpu.HBM), pl.BlockSpec(memory_space=pltpu.VMEM)
    inputs = (routes.reshape(1, pairs), probs.reshape(1, pairs), acts, cotangent)
    mix, *sent = pl.pallas_call(
        functools.partial(pack_kernel, experts, capacity, top),
        in_specs=[far_off] * 4,
        out_specs=[vmem] * (1 + experts),
        out_shape=[pltpu.VMEM((2, token_count, LANES), jnp.float32)] + [block] * experts,
        scratch_shapes=[pltpu.VMEM(x.shape, x.dtype) for x in inputs[:2]]
        + [pltpu.VMEM((2 * token_count, width), acts.dtype), pltpu.SemaphoreType.DMA((4,))],
        compiler_params=room(4),
        name="pack",
    )(*map(in_hbm, inputs))

    members = [(half, by) for half in range(2) for by in range(r)]
    near = [sent[0]]
    got = [to_expert(sent[k], k) for k in range(1, experts)]
    near += [to_member(sent[0], half, by) for half, by in members[1:]]
    got = got[0] if experts == 2 else jnp.concatenate(got, axis=0)
    far = [got] + [to_member(got, half, by) for half, by in members[1:]]
    weights = (w_gate.reshape(width, hidden), w_up.reshape(width, hidden), w_down.reshape(hidden, width))
    tall = experts * 2 * r * (-(-capacity // TILE)) * TILE
    count = len(members)
    laid = pltpu.VMEM((tall, width), jnp.bfloat16)
    acts_rows, cot_rows, *held = pl.pallas_call(
        functools.partial(near_kernel, capacity, count),
        in_specs=[far_off] * 3 + [vmem] * count,
        out_specs=[vmem] * 5,
        out_shape=[laid] * 2 + [pltpu.VMEM(w.shape, w.dtype) for w in weights],
        scratch_shapes=[pltpu.SemaphoreType.DMA((3,))],
        compiler_params=room(4),
        name="near",
    )(*map(in_hbm, weights), *map(near_core, near))
    *parts, _, _ = pl.pallas_call(
        functools.partial(expert_kernel, capacity, count),
        in_specs=[vmem] * (5 + count),
        out_specs=[vmem] * (2 * count + 2),
        out_shape=[block] * count + [rest] * count + [laid] * 2,
        input_output_aliases={3: 2 * count, 4: 2 * count + 1},
        compiler_params=room(8),
        name="expert",
    )(*map(near_core, (*held, acts_rows, cot_rows, far[0], *far[:0:-1])))
    near, far = parts[:count], parts[count:]
    far = [far[0]] + [to_member(x, half, -by) for x, (half, by) in zip(far[:0:-1], members[:0:-1])]
    near = [near[0]] + [to_member(x, half, -by) for x, (half, by) in zip(near[1:], members[1:])]
    total = pl.pallas_call(sum_kernel, out_shape=rest, compiler_params=room(4), name="total")(*map(near_core, far))
    back = [to_expert(total[(k - 1) * tiles : k * tiles], -k) for k in range(1, experts)]
    layer_out, section_grad = [
        pl.pallas_call(
            functools.partial(finish_kernel, which, capacity, count),
            in_specs=[pl.BlockSpec(memory_space=pltpu.SMEM)] + [vmem] * (2 + count + len(back)),
            out_shape=shape(acts.shape, jnp.bfloat16) if which == 0 else pltpu.VMEM(acts.shape, jnp.bfloat16),
            compiler_params=room(4),
            name=name,
        )(keep, *map(near_core, (mix, base, *near, *back)))
        for which, name, base in ((0, "out", acts), (1, "grad", cotangent))
    ]
    return layer_out, to_below(section_grad)


def solution(mesh):
    rows = P(("pipe", "expert", "dp"), None)
    return jax.shard_map(
        shards,
        mesh=mesh,
        in_specs=(
            rows,
            rows,
            rows,
            rows,
            P("pipe", ("expert", "dp")),
            P("pipe", "expert", None, "dp"),
            P("pipe", "expert", None, "dp"),
            P("pipe", "expert", "dp", None),
        ),
        out_specs=(rows, rows),
        check_vma=False,
    )
```
